32 devices in a mesh: group: 4 (over x, core), ep: 8 (over z, y).
Axes of the slice: x: 2, y: 2, z: 4, core: 2. Of those that a mesh axis runs over, the one named last changes fastest.
Arguments:
- tokens: bfloat16 [4096, 4096], P(('group', 'ep')), may hold values from -6 to 6
- out_grad: bfloat16 [4096, 4096], P(('group', 'ep')), may hold values from -6 to 6
- routes: int32 [4096, 2], P(('group', 'ep')), may hold values from 0 to 63, all different within a row; in each aligned block of 128 rows (0 to 127, 128 to 255, ...) at most 5 rows name the same one
- gate_probs: float32 [4096, 2], P(('group', 'ep')), may hold values from 0.1 to 1
- hot: int32 [1], replicated, may hold values from 0 to 65535
- gate_weight: bfloat16 [4, 4096, 11008], P('group', None, 'ep'), may hold values from -0.09375 to 0.09375
- up_weight: bfloat16 [4, 4096, 11008], P('group', None, 'ep'), may hold values from -0.09375 to 0.09375
- down_weight: bfloat16 [4, 11008, 4096], P('group', 'ep'), may hold values from -0.0546875 to 0.0546875
Outputs:
- tokens_grad: bfloat16 [4096, 4096], P(('group', 'ep'))
- gate_weight_grad: bfloat16 [4, 4096, 11008], P('group', None, 'ep')
- up_weight_grad: bfloat16 [4, 4096, 11008], P('group', None, 'ep')
- down_weight_grad: bfloat16 [4, 11008, 4096], P('group', 'ep')
The draws below stay inside these ranges and needn't reach their ends.
Inputs may be any that keep to these rules, and one draw needn't show every extreme that they name: `routes`: each row names two different experts. Among the 128 rows of one device, at most 5 name the same expert.
All inputs are finite; a program needn't handle non-finite values.
Results may differ from the reference program's by a relative error of at most 0.024.
Values may be sent and summed in bfloat16 or wider, within the bound.
No kernel may reach another device: no remote copies, remote signals or barrier semaphores. Data moves between devices by JAX's collectives and lax.ppermute only.
A program may use at most 448 MiB of HBM per device.

```python
import math
from functools import partial
import jax
import jax.numpy as jnp
import numpy as np
from jax import lax

D = 4096
FF = 11008
EXPERTS_ALL = 64
TOK_DEV = 128
EXPERTS = 4
CAP = 5
COLD_CAP = 3
TOKENS = 4096
N_GROUP = 4


def block_scale(key, dims, cuts, low, largest):
    gain = 1.0
    for dim, blocks in cuts:
        steps = jax.random.uniform(jax.random.fold_in(jax.random.fold_in(key, 6), dim), (blocks,), jnp.float32, low / len(cuts), largest / len(cuts))
        gain = gain * jnp.repeat(jnp.exp(steps), dims[dim] // blocks).reshape((-1,) + (1,) * (len(dims) - 1 - dim))
    return gain


def shared_out(rng, own, number, rows, count, top, reach, skew):
    order = jax.random.permutation(rng, count)
    packed, usual = portions_of(count, rows * top, reach, skew, True), portions_of(count, rows * top, reach, skew, False)
    places = jnp.arange(count)

    def named(lengths, rotation):
        used = int((lengths > 0).sum())
        fixed = max(1, used // 4)
        shifted = fixed + (places - fixed + rotation * (used - fixed)) % max(1, count - fixed)
        return jnp.zeros((count,), jnp.int32).at[order[jnp.where(places < fixed, places, shifted)]].set(jnp.asarray(lengths, jnp.int32))

    lengths = jnp.where(number % 4 == 0, named(packed, number // 4), named(usual, number - number // 4 - 1))
    mixed = jax.random.permutation(jax.random.fold_in(own, 3), count)
    donor, receiver = mixed[0:count // 2 * 2:2], mixed[1:count // 2 * 2:2]
    margin = jnp.minimum(lengths[donor] - 1, reach - lengths[receiver]) // 2
    margin = jnp.where((donor == order[0]) | (receiver == order[0]) | (lengths[receiver] == 0), 0, jnp.maximum(margin, 0))
    shifted = jax.random.randint(jax.random.fold_in(own, 4), (count // 2,), 0, 1 << 20) % (margin + 1)
    lengths = lengths.at[donor].add(-shifted).at[receiver].add(shifted)
    members = jnp.searchsorted(jnp.cumsum(lengths), jnp.arange(rows * top), side="right").astype(jnp.int32)
    grid = members.reshape(top, rows).T
    grid = grid[jax.random.permutation(jax.random.fold_in(own, 1), rows)]
    rotation = jax.random.randint(jax.random.fold_in(own, 2), (rows, 1), 0, top)
    return jnp.take_along_axis(grid, (jnp.arange(top)[None, :] + rotation) % top, axis=1)


def portions_of(count, total, reach, lean, full):
    weights = [(1 << 20) // math.isqrt(rank ** lean) + 1 for rank in range(1, count + 1)]
    largest = reach if full else min(reach, max(-(-total // count), total * weights[0] // sum(weights)))
    least = 1 if total - largest >= count - 1 else 0
    counts, spare = [largest] + [least] * (count - 1), total - largest - least * (count - 1)
    while spare > 0:
        candidates = [i for i in range(1, count) if counts[i] < largest] or [i for i in range(1, count) if counts[i] < reach]
        mass, left = sum([weights[i] for i in candidates]), spare
        for i in candidates:
            addition = min(reach - counts[i], max(1, left * weights[i] // mass), spare)
            counts[i] = counts[i] + addition
            spare = spare - addition
    return np.array(counts)


def gaussian(key, extent, scale, bound, shards=(), held_as=jnp.bfloat16):
    factor_of = block_scale(key, extent, shards, -0.22, 0.18) if shards else 1.0
    result = jax.random.normal(key, extent, jnp.float32) * scale * factor_of
    return jnp.minimum(jnp.maximum(result, -bound), bound).astype(held_as)


def setup_inputs(seed: int = 0) -> dict:
    splits = jax.random.split(jax.random.key(seed), 9)
    tokens = gaussian(splits[0], (TOKENS, D), 1.0, 6.0, ((0, 32),))
    out_grad = gaussian(splits[1], (TOKENS, D), 1.0, 6.0, ((0, 32),))
    routes_keys = jax.random.split(jax.random.fold_in(splits[2], 1), TOKENS // TOK_DEV)
    routes_turns = jax.random.permutation(jax.random.fold_in(splits[2], 3), TOKENS // TOK_DEV)
    routes = jax.vmap(lambda own, number: shared_out(jax.random.fold_in(splits[2], 2), own, number, TOK_DEV, EXPERTS_ALL, 2, CAP, 1))(routes_keys, routes_turns).reshape((TOKENS, 2))
    gate_probs = jnp.clip(jnp.exp(math.log(1.0) - 2.3025851 * jax.random.uniform(splits[3], (TOKENS, 2), jnp.float32) ** block_scale(splits[3], (TOKENS, 2), ((0, 32),), -0.2, 0.2)), 0.1, 1.0)
    hot = jax.random.randint(splits[4], (1,), 0, 65536).astype(jnp.int32)
    gate_weight = gaussian(splits[5], (EXPERTS, D, FF), D ** -0.5, 0.09375, ((0, 4), (2, 8)))
    up_weight = gaussian(splits[6], (EXPERTS, D, FF), D ** -0.5, 0.09375, ((0, 4), (2, 8)))
    down_weight = gaussian(splits[7], (EXPERTS, FF, D), FF ** -0.5, 0.0546875, ((0, 4), (1, 8)))
    return dict(tokens=tokens, out_grad=out_grad, routes=routes, gate_probs=gate_probs, hot=hot, gate_weight=gate_weight, up_weight=up_weight, down_weight=down_weight)


def slot_map(route_block, prob_block, experts, capacity):
    expert_index = jnp.arange(experts, dtype=jnp.int32)
    named_hits = route_block[None, :, :] == expert_index[:, None, None]
    weight_sum = jnp.sum(jnp.where(named_hits, prob_block[None, :, :], 0.0), axis=2)
    chosen = jnp.any(named_hits, axis=2).astype(jnp.int32)
    position = jnp.cumsum(chosen, axis=1) - 1
    slot_index = jnp.arange(capacity, dtype=jnp.int32)
    onehot = ((position[:, None, :] == slot_index[None, :, None]) & (chosen[:, None, :] == 1)).astype(jnp.float32)
    slot_weight = jnp.sum(onehot * weight_sum[:, None, :], axis=2)
    return onehot, slot_weight


def settle(partial_term, rounded):
    narrowed = lax.optimization_barrier(partial_term.astype(jnp.bfloat16)).astype(partial_term.dtype)
    return jnp.where(rounded, narrowed, partial_term)


def expert_backward(token_rows, signal_rows, gate_w, up_w, down_w):
    gate_pre = jnp.dot(token_rows, gate_w, preferred_element_type=jnp.float32)
    up_pre = jnp.dot(token_rows, up_w, preferred_element_type=jnp.float32)
    logistic = jax.nn.sigmoid(gate_pre)
    swished = gate_pre * logistic
    hidden = (swished * up_pre).astype(jnp.bfloat16)
    hidden_grad = jnp.dot(signal_rows, down_w.T, preferred_element_type=jnp.float32)
    gate_signal = (hidden_grad * up_pre * logistic * (1.0 + gate_pre * (1.0 - logistic))).astype(jnp.bfloat16)
    up_signal = (hidden_grad * swished).astype(jnp.bfloat16)
    grad_down = jnp.dot(hidden.T, signal_rows, preferred_element_type=jnp.float32)
    grad_gate = jnp.dot(token_rows.T, gate_signal, preferred_element_type=jnp.float32)
    grad_up = jnp.dot(token_rows.T, up_signal, preferred_element_type=jnp.float32)
    token_grad = jnp.dot(gate_signal, gate_w.T, preferred_element_type=jnp.float32) + jnp.dot(up_signal, up_w.T, preferred_element_type=jnp.float32)
    return grad_gate, grad_up, grad_down, token_grad


def expert_total(operands):
    token_groups, signal_groups, gate_w, up_w, down_w, rounded = operands

    def per_group(totals, rows):
        grad_gate, grad_up, grad_down, token_grad = expert_backward(rows[0], rows[1], gate_w, up_w, down_w)
        pieces = (grad_gate, grad_up, grad_down)
        updated = tuple(total + settle(piece, rounded) for total, piece in zip(totals, pieces))
        return updated, token_grad

    zeros = (jnp.zeros(gate_w.shape, jnp.float32), jnp.zeros(up_w.shape, jnp.float32), jnp.zeros(down_w.shape, jnp.float32))
    totals, token_grads = lax.scan(per_group, zeros, (token_groups, signal_groups))
    return totals[0].astype(jnp.bfloat16), totals[1].astype(jnp.bfloat16), totals[2].astype(jnp.bfloat16), token_grads


def reference(tokens, out_grad, routes, gate_probs, hot, gate_weight, up_weight, down_weight):
    blocks = tokens.shape[0] // TOK_DEV
    width = tokens.shape[1]
    hot_expert = jnp.remainder(hot[0], EXPERTS).astype(jnp.int32)
    mapper = jax.vmap(partial(slot_map, experts=EXPERTS, capacity=CAP))
    onehot, slot_weight = mapper(routes.reshape(blocks, TOK_DEV, 2), gate_probs.reshape(blocks, TOK_DEV, 2))
    is_hot = jnp.arange(EXPERTS, dtype=jnp.int32) == hot_expert
    retained = (is_hot[:, None] | (jnp.arange(CAP, dtype=jnp.int32)[None, :] < COLD_CAP)).astype(jnp.float32)
    onehot = onehot * retained[None, :, :, None]
    slot_weight = slot_weight * retained[None, :, :]
    token_blocks = tokens.reshape(blocks, TOK_DEV, width).astype(jnp.float32)
    signal_blocks = out_grad.reshape(blocks, TOK_DEV, width).astype(jnp.float32)
    token_slots = jnp.einsum('best,btd->ebsd', onehot, token_blocks, precision=lax.Precision.HIGHEST).astype(jnp.bfloat16)
    picked = jnp.einsum('best,btd->ebsd', onehot, signal_blocks, precision=lax.Precision.HIGHEST)
    signal_slots = (jnp.transpose(slot_weight, (1, 0, 2))[:, :, :, None] * picked).astype(jnp.bfloat16)
    group_rows = (blocks // N_GROUP) * CAP
    grad_gate, grad_up, grad_down, token_grad = lax.map(expert_total, (token_slots.reshape(EXPERTS, N_GROUP, group_rows, width), signal_slots.reshape(EXPERTS, N_GROUP, group_rows, width), gate_weight, up_weight, down_weight, is_hot))
    grad_slots = token_grad.reshape(EXPERTS, blocks, CAP, width)
    summed = jnp.einsum('best,ebsd->btd', onehot, grad_slots, precision=lax.Precision.HIGHEST)
    tokens_grad = summed.reshape(blocks * TOK_DEV, width).astype(jnp.bfloat16)
    return tokens_grad, grad_gate, grad_up, grad_down
```

```python
import functools

import jax
import jax.numpy as jnp
import numpy as np
from jax import lax
from jax.experimental import pallas as pl
from jax.experimental.pallas import tpu as pltpu
from jax.sharding import PartitionSpec as P

CAP = 5
COLD_CAP = 3

NT = (((1,), (1,)), ((), ()))
TN = (((0,), (0,)), ((), ()))
NN = (((1,), (0,)), ((), ()))


def mm(left, right, dims):
    return lax.dot_general(left, right, dims, preferred_element_type=jnp.float32)


def tile_of(inner, limit=344):
    fits = [t for t in range(8, limit + 1, 8) if inner % t == 0]
    return fits[-1] if fits else inner


def slot_map(route_block, prob_block, expert_index, capacity):
    named_hits = route_block[None, :, :] == expert_index[:, None, None]
    weight_sum = jnp.sum(jnp.where(named_hits, prob_block[None, :, :], 0.0), axis=2)
    chosen = jnp.any(named_hits, axis=2).astype(jnp.int32)
    position = jnp.cumsum(chosen, axis=1) - 1
    slot_index = jnp.arange(capacity, dtype=jnp.int32)
    onehot = (
        (position[:, None, :] == slot_index[None, :, None]) & (chosen[:, None, :] == 1)
    ).astype(jnp.float32)
    slot_weight = jnp.sum(onehot * weight_sum[:, None, :], axis=2)
    return (onehot, slot_weight)


def full(shape):
    return pl.BlockSpec(shape, lambda i: (0,) * len(shape), pipeline_mode=pl.Buffered(1))


def rows_of(tile, width):
    return pl.BlockSpec((tile, width), lambda i: (i, 0))


def masks_of(bits):
    masks = [0]
    for bit in bits:
        masks = masks + [m | (1 << bit) for m in masks]
    return masks


def split_kernel(order, block, chunk, perm_ref, a0_ref, a1_ref, b0_ref, b1_ref, t_ref, s_ref):
    perm = perm_ref[...]
    half = a0_ref.shape[1]
    pair = 2 * block
    per = a0_ref.shape[0] // pair
    count = 2 * per
    for side, refs in enumerate(((a0_ref, a1_ref), (b0_ref, b1_ref))):
        cols = slice(side * half, (side + 1) * half)
        for first in range(0, count, chunk):
            pieces = []
            for at in range(first, first + chunk):
                src = at if side == 0 else order[at]
                pieces.append(refs[src // per][(src % per) * pair : (src % per + 1) * pair, :])
            mixed = mm(perm, jnp.concatenate(pieces, axis=0), NN).astype(jnp.bfloat16)
            rows = slice(first * block, (first + chunk) * block)
            t_ref[rows, cols] = mixed[: chunk * block]
            s_ref[rows, cols] = mixed[chunk * block :]


def split_call(a0, a1, b0, b1, order, block):
    rows, half = a0.shape
    chunk = min(4, 2 * rows // (2 * block))
    size = 2 * block * chunk
    perm = np.zeros((size, size), np.float32)
    for side in range(2):
        for row in range(chunk * block):
            blk, rest = divmod(row, block)
            src, slot = divmod(rest, CAP)
            perm[side * chunk * block + row, blk * 2 * block + src * 2 * CAP + side * CAP + slot] = 1.0
    out = jax.ShapeDtypeStruct((rows, 2 * half), jnp.bfloat16)
    return pl.pallas_call(
        functools.partial(split_kernel, order, block, chunk),
        out_shape=[out, out],
        cost_estimate=pl.CostEstimate(flops=16 * rows * half * size // 4, bytes_accessed=16 * rows * half, transcendentals=0),
    )(jnp.asarray(perm, jnp.bfloat16), a0, a1, b0, b1)


def pre_kernel(t_ref, wg_ref, wu_ref, pg_ref, pu_ref):
    t = t_ref[...]
    pg_ref[...] = mm(wg_ref[...], t, NT)
    pu_ref[...] = mm(wu_ref[...], t, NT)


def pre_call(t, wg, wu):
    inner, width = wg.shape
    rows = t.shape[0]
    tile = tile_of(inner)
    return pl.pallas_call(
        pre_kernel,
        grid=(inner // tile,),
        in_specs=[full((rows, width)), rows_of(tile, width), rows_of(tile, width)],
        out_specs=[rows_of(tile, rows)] * 2,
        out_shape=[jax.ShapeDtypeStruct((inner, rows), jnp.float32)] * 2,
        cost_estimate=pl.CostEstimate(
            flops=4 * inner * width * rows, bytes_accessed=4 * inner * width, transcendentals=0
        ),
    )(t, wg, wu)


def signal_kernel(
    perm_ref, s_ref, wg_ref, wu_ref, wd_ref, pg_ref, pu_ref, h_ref, gs_ref, us_ref, dxa_ref, dxb_ref, acc_ref
):
    step = pl.program_id(0)
    gate = pg_ref[...]
    up = pu_ref[...]
    logistic = jax.nn.sigmoid(gate)
    swished = gate * logistic
    h_ref[...] = (swished * up).astype(jnp.bfloat16)
    hidden_grad = mm(wd_ref[...], s_ref[...], NT)
    gs = (hidden_grad * up * logistic * (1.0 + gate * (1.0 - logistic))).astype(jnp.bfloat16)
    us = (hidden_grad * swished).astype(jnp.bfloat16)
    gs_ref[...] = gs
    us_ref[...] = us
    part = mm(gs, wg_ref[...], TN) + mm(us, wu_ref[...], TN)

    @pl.when(step == 0)
    def _():
        acc_ref[...] = part

    @pl.when(step > 0)
    def _():
        acc_ref[...] += part

    @pl.when(step == pl.num_programs(0) - 1)
    def _():
        half = dxa_ref.shape[1]
        dxa_ref[...] = acc_ref[:, :half].astype(jnp.bfloat16)
        late = acc_ref[:, half:].astype(jnp.bfloat16)
        dxb_ref[...] = mm(perm_ref[...], late, NN).astype(jnp.bfloat16)


def signal_call(perm, s, wg, wu, wd, pg, pu):
    inner, width = wg.shape
    rows = s.shape[0]
    tile = tile_of(inner)
    return pl.pallas_call(
        signal_kernel,
        grid=(inner // tile,),
        in_specs=[full((rows, rows)), full((rows, width))] + [rows_of(tile, width)] * 3 + [rows_of(tile, rows)] * 2,
        out_specs=[rows_of(tile, rows)] * 3 + [full((rows, width // 2))] * 2,
        out_shape=[jax.ShapeDtypeStruct((inner, rows), jnp.bfloat16)] * 3
        + [jax.ShapeDtypeStruct((rows, width // 2), jnp.bfloat16)] * 2,
        scratch_shapes=[pltpu.VMEM((rows, width), jnp.float32)],
        cost_estimate=pl.CostEstimate(
            flops=6 * inner * width * rows, bytes_accessed=6 * inner * width, transcendentals=inner * rows
        ),
    )(perm, s, wg, wu, wd, pg, pu)


def weight_kernel(t_ref, s_ref, h_ref, gs_ref, us_ref, gg_ref, gu_ref, gd_ref):
    t = t_ref[...]
    gg_ref[...] = mm(gs_ref[...], t, NN).astype(jnp.bfloat16)
    gu_ref[...] = mm(us_ref[...], t, NN).astype(jnp.bfloat16)
    gd_ref[...] = mm(h_ref[...], s_ref[...], NN).astype(jnp.bfloat16)


def weight_call(t, s, h, gs, us):
    inner, rows = h.shape
    width = t.shape[1]
    tile = tile_of(inner)
    return pl.pallas_call(
        weight_kernel,
        grid=(inner // tile,),
        in_specs=[full((rows, width))] * 2 + [rows_of(tile, rows)] * 3,
        out_specs=[rows_of(tile, width)] * 3,
        out_shape=[jax.ShapeDtypeStruct((inner, width), jnp.bfloat16)] * 3,
        cost_estimate=pl.CostEstimate(
            flops=6 * inner * width * rows, bytes_accessed=6 * inner * width, transcendentals=0
        ),
    )(t, s, h, gs, us)


def swap(value, axis, size, offset):
    return lax.ppermute(value, axis, [(i, i ^ offset) for i in range(size)])


def per_device(tokens, out_grad, routes, gate_probs, hot, gate_weight, up_weight, down_weight):
    groups = lax.axis_size("group")
    slices = lax.axis_size("ep")
    width = tokens.shape[1]
    half = width // 2
    block = groups * CAP
    bits = slices.bit_length() - 1
    order_a = list(range(bits - 1, -1, -1))
    order_b = [0] + list(range(bits - 1, 0, -1))
    masks_a, masks_b = masks_of(order_a), masks_of(order_b)

    experts = jnp.arange(groups, dtype=jnp.int32) ^ lax.axis_index("group")
    onehot, slot_weight = slot_map(routes, gate_probs, experts, CAP)
    hot_id = jnp.remainder(hot[0], groups)
    slot_ids = jnp.arange(CAP, dtype=jnp.int32)
    retained = ((experts == hot_id)[:, None] | (slot_ids[None, :] < COLD_CAP)).astype(jnp.float32)
    pick = onehot * retained[:, :, None]
    weight = slot_weight * retained
    picker = pick.astype(jnp.bfloat16)
    token_slots = jnp.einsum("est,td->esd", picker, tokens, preferred_element_type=jnp.float32).astype(jnp.bfloat16)
    picked = jnp.einsum("est,td->esd", picker, out_grad, preferred_element_type=jnp.float32)
    signal_slots = (weight[:, :, None] * picked).astype(jnp.bfloat16)
    slots = jnp.concatenate([token_slots, signal_slots], axis=1)

    own = jnp.concatenate([slots[0]] + [swap(slots[k], "group", groups, k) for k in range(1, groups)], axis=0)

    held_a, held_b = own[:, :half], own[:, half:]
    for stage in range(bits):
        got_a = swap(held_a, "ep", slices, 1 << order_a[stage])
        got_b = swap(held_b, "ep", slices, 1 << order_b[stage])
        if stage < bits - 1:
            held_a = jnp.concatenate([held_a, got_a], axis=0)
            held_b = jnp.concatenate([held_b, got_b], axis=0)
    back = [masks_b.index(m) for m in masks_a]
    t, s = split_call(held_a, got_a, held_b, got_b, back, block)

    wg = jnp.swapaxes(gate_weight[0], 0, 1)
    wu = jnp.swapaxes(up_weight[0], 0, 1)
    wd = down_weight[0]
    pg, pu = pre_call(t, wg, wu)
    perm = np.zeros((slices * block,) * 2, np.float32)
    for at, mask in enumerate(masks_b):
        for row in range(block):
            perm[at * block + row, masks_a.index(mask) * block + row] = 1.0
    h, gs, us, dxa, dxb = signal_call(jnp.asarray(perm, jnp.bfloat16), s, wg, wu, wd, pg, pu)
    gg, gu, gd = weight_call(t, s, h, gs, us)

    for stage in range(bits - 1, -1, -1):
        sums = []
        for value, order in ((dxa, order_a), (dxb, order_b)):
            keep, send = value[: value.shape[0] // 2], value[value.shape[0] // 2 :]
            got = swap(send, "ep", slices, 1 << order[stage])
            sums.append((keep.astype(jnp.float32) + got.astype(jnp.float32)).astype(jnp.bfloat16))
        dxa, dxb = sums
    mine = jnp.concatenate([dxa, dxb], axis=1).reshape(groups, CAP, width)
    returned = jnp.stack([mine[0]] + [swap(mine[k], "group", groups, k) for k in range(1, groups)])
    tokens_grad = jnp.einsum("est,esd->td", picker, returned, preferred_element_type=jnp.float32).astype(jnp.bfloat16)
    return (tokens_grad, jnp.swapaxes(gg, 0, 1)[None], jnp.swapaxes(gu, 0, 1)[None], gd[None])


def solution(mesh):
    in_specs = (
        P(("group", "ep"), None),
        P(("group", "ep"), None),
        P(("group", "ep"), None),
        P(("group", "ep"), None),
        P(),
        P("group", None, "ep"),
        P("group", None, "ep"),
        P("group", "ep", None),
    )
    out_specs = (
        P(("group", "ep"), None),
        P("group", None, "ep"),
        P("group", None, "ep"),
        P("group", "ep", None),
    )
    return jax.shard_map(per_device, mesh=mesh, in_specs=in_specs, out_specs=out_specs, check_vma=False)
```

```python
import functools

import jax
import jax.numpy as jnp
import numpy as np
from jax import lax
from jax.experimental import pallas as pl
from jax.experimental.pallas import tpu as pltpu
from jax.sharding import PartitionSpec as P

CAP = 5
COLD_CAP = 3
SLOTS = 3
STEP = 512
BANDS = 4
SMALL_MIB = 12
SPARE_MIB = 16

NT = (((1,), (1,)), ((), ()))
TN = (((0,), (0,)), ((), ()))
NN = (((1,), (0,)), ((), ()))


def mm(left, right, dims):
    return lax.dot_general(left, right, dims, preferred_element_type=jnp.float32)


def tile_of(inner, limit=344):
    fits = [t for t in range(8, limit + 1, 8) if inner % t == 0]
    return fits[-1] if fits else inner


def slot_map(route_block, prob_block, expert_index, capacity):
    named_hits = route_block[None, :, :] == expert_index[:, None, None]
    weight_sum = jnp.sum(jnp.where(named_hits, prob_block[None, :, :], 0.0), axis=2)
    chosen = jnp.any(named_hits, axis=2).astype(jnp.int32)
    position = jnp.cumsum(chosen, axis=1) - 1
    slot_index = jnp.arange(capacity, dtype=jnp.int32)
    onehot = (
        (position[:, None, :] == slot_index[None, :, None]) & (chosen[:, None, :] == 1)
    ).astype(jnp.float32)
    slot_weight = jnp.sum(onehot * weight_sum[:, None, :], axis=2)
    return (onehot, slot_weight)


def full(shape):
    return pl.BlockSpec(shape, lambda i: (0,) * len(shape), pipeline_mode=pl.Buffered(1))


def rows_of(tile, width):
    return pl.BlockSpec((tile, width), lambda i: (i, 0))


def masks_of(bits):
    masks = [0]
    for bit in bits:
        masks = masks + [m | (1 << bit) for m in masks]
    return masks


def join(perm, refs):
    a0, a1, b0, b1 = (ref[...] for ref in refs)
    late = mm(perm, jnp.concatenate([b0, b1], axis=0), NN).astype(jnp.bfloat16)
    return jnp.concatenate([jnp.concatenate([a0, a1], axis=0), late], axis=1)


def cuts_of(inner, step):
    return [(low, min(low + step, inner)) for low in range(0, inner, step)]


VMEM = pl.BlockSpec(memory_space=pltpu.VMEM)
ANY = pl.BlockSpec(memory_space=pl.ANY)


def load_kernel(cuts, w_hbm, w_ref, sems):
    copies = []
    for at, (low, high) in enumerate(cuts):
        rows = pl.ds(low, high - low)
        copies.append(pltpu.make_async_copy(w_hbm.at[rows, :], w_ref.at[rows, :], sems.at[at]))
        copies[at].start()
    for copy in copies:
        copy.wait()


def load_call(w, before):
    size = 2 * w.size
    grant = (63 << 20) - (before + 1) * size - min(6 << 20, size // 2)
    cuts = cuts_of(w.shape[0], 344)
    return pl.pallas_call(
        functools.partial(load_kernel, cuts),
        in_specs=[pl.BlockSpec(memory_space=pltpu.HBM)],
        out_specs=VMEM,
        out_shape=pltpu.VMEM(w.shape, w.dtype),
        scratch_shapes=[pltpu.SemaphoreType.DMA((len(cuts),))],
        compiler_params=pltpu.CompilerParams(vmem_limit_bytes=grant),
        cost_estimate=pl.CostEstimate(flops=0, bytes_accessed=2 * w.size, transcendentals=0),
    )(w)


def gate_kernel(cuts, perm_ref, a0_ref, a1_ref, b0_ref, b1_ref, wg_ref, t_ref, pg_ref):
    t = join(perm_ref[...], (a0_ref, a1_ref, b0_ref, b1_ref))
    t_ref[...] = t
    for low, high in cuts:
        pg_ref[low:high, :] = mm(wg_ref[low:high, :], t, NT)


def gate_call(perm, parts, wg):
    inner, width = wg.shape
    rows = perm.shape[0]
    return pl.pallas_call(
        functools.partial(gate_kernel, cuts_of(inner, STEP)),
        in_specs=[VMEM] * 6,
        out_specs=[VMEM] * 2,
        out_shape=[
            jax.ShapeDtypeStruct((rows, width), jnp.bfloat16),
            jax.ShapeDtypeStruct((inner, rows), jnp.float32),
        ],
        compiler_params=pltpu.CompilerParams(vmem_limit_bytes=SMALL_MIB << 20),
        cost_estimate=pl.CostEstimate(
            flops=2 * inner * width * rows, bytes_accessed=2 * inner * width, transcendentals=0
        ),
    )(perm, *parts, wg)


def up_kernel(cuts, t_ref, wu_ref, pu_ref):
    t = t_ref[...]
    for low, high in cuts:
        pu_ref[low:high, :] = mm(wu_ref[low:high, :], t, NT)


def up_call(t, wu):
    inner, width = wu.shape
    rows = t.shape[0]
    return pl.pallas_call(
        functools.partial(up_kernel, cuts_of(inner, STEP)),
        in_specs=[VMEM] * 2,
        out_specs=VMEM,
        out_shape=jax.ShapeDtypeStruct((inner, rows), jnp.float32),
        compiler_params=pltpu.CompilerParams(vmem_limit_bytes=SMALL_MIB << 20),
        cost_estimate=pl.CostEstimate(
            flops=2 * inner * width * rows, bytes_accessed=2 * inner * width, transcendentals=0
        ),
    )(t, wu)


def signal_kernel(
    cuts, perm_ref, back_ref, a0_ref, a1_ref, b0_ref, b1_ref, pg_ref, pu_ref, wg_ref, wu_hbm, wd_hbm,
    s_ref, h_ref, gs_ref, us_ref, keepa_ref, senda_ref, keepb_ref, sendb_ref, acc_ref, wu_ref, wd_ref, sems,
):
    copies = []
    for side, (src, dst) in enumerate(((wd_hbm, wd_ref), (wu_hbm, wu_ref))):
        for at, (low, high) in enumerate(cuts):
            rows = pl.ds(low, high - low)
            copies.append(pltpu.make_async_copy(src.at[rows, :], dst.at[rows, :], sems.at[side, at]))
    for copy in copies[: len(cuts)]:
        copy.start()
    s = join(perm_ref[...], (a0_ref, a1_ref, b0_ref, b1_ref))
    s_ref[...] = s
    for at, (low, high) in enumerate(cuts):
        gate = pg_ref[low:high, :]
        up = pu_ref[low:high, :]
        logistic = jax.nn.sigmoid(gate)
        swished = gate * logistic
        h_ref[low:high, :] = (swished * up).astype(jnp.bfloat16)
        copies[at].wait()
        copies[len(cuts) + at].start()
        hidden_grad = mm(wd_ref[low:high, :], s, NT)
        gs_ref[low:high, :] = (hidden_grad * up * logistic * (1.0 + gate * (1.0 - logistic))).astype(jnp.bfloat16)
        us_ref[low:high, :] = (hidden_grad * swished).astype(jnp.bfloat16)
    half = keepa_ref.shape[1]
    kept = keepa_ref.shape[0]
    wide = 2 * half // BANDS
    bands = [slice(band * wide, (band + 1) * wide) for band in range(BANDS)]
    gs = gs_ref[...].T
    for cols in bands:
        acc_ref[:, cols] = mm(gs, wg_ref[:, cols], NN)
    us = us_ref[...].T
    for copy in copies[len(cuts) :]:
        copy.wait()
    for cols in bands:
        part = (acc_ref[:, cols] + mm(us, wu_ref[:, cols], NN)).astype(jnp.bfloat16)
        if cols.start < half:
            keepa_ref[:, cols] = part[:kept]
            senda_ref[:, cols] = part[kept:]
        else:
            there = slice(cols.start - half, cols.stop - half)
            late = mm(back_ref[...], part, NN).astype(jnp.bfloat16)
            keepb_ref[:, there] = late[:kept]
            sendb_ref[:, there] = late[kept:]


def signal_call(perm, back, parts, pg, pu, wg, wu, wd):
    inner, width = wg.shape
    rows = perm.shape[0]
    cuts = cuts_of(inner, 256)
    grant = (63 << 20) - 2 * wg.size - (SPARE_MIB << 20)
    return pl.pallas_call(
        functools.partial(signal_kernel, cuts),
        in_specs=[VMEM] * 9 + [ANY] * 2,
        out_specs=[VMEM] * 8,
        out_shape=[jax.ShapeDtypeStruct((rows, width), jnp.bfloat16)]
        + [jax.ShapeDtypeStruct((inner, rows), jnp.bfloat16)] * 3
        + [jax.ShapeDtypeStruct((rows // 2, width // 2), jnp.bfloat16)] * 4,
        scratch_shapes=[
            pltpu.VMEM((rows, width), jnp.float32),
            pltpu.VMEM((inner, width), jnp.bfloat16),
            pltpu.VMEM((inner, width), jnp.bfloat16),
            pltpu.SemaphoreType.DMA((2, len(cuts))),
        ],
        compiler_params=pltpu.CompilerParams(vmem_limit_bytes=grant),
        cost_estimate=pl.CostEstimate(
            flops=6 * inner * width * rows, bytes_accessed=6 * inner * width, transcendentals=inner * rows
        ),
    )(perm, back, *parts, pg, pu, wg, wu, wd)


def weight_kernel(cuts, x_ref, g_ref, out_hbm, buf_ref, sems):
    x = x_ref[...]
    copies = []
    for at, (low, high) in enumerate(cuts):
        slot = at % SLOTS
        if at >= SLOTS:
            copies[at - SLOTS].wait()
        size = high - low
        buf_ref[slot, :size, :] = mm(g_ref[low:high, :], x, NN).astype(jnp.bfloat16)
        copies.append(
            pltpu.make_async_copy(buf_ref.at[slot, pl.ds(0, size), :], out_hbm.at[pl.ds(low, size), :], sems.at[slot])
        )
        copies[at].start()
    for copy in copies[max(0, len(copies) - SLOTS) :]:
        copy.wait()


def weight_call(x, g):
    inner, rows = g.shape
    width = x.shape[1]
    step = min(256, inner)
    cuts = cuts_of(inner, step)
    return pl.pallas_call(
        functools.partial(weight_kernel, cuts),
        in_specs=[pl.BlockSpec(memory_space=pltpu.VMEM)] * 2,
        out_specs=pl.BlockSpec(memory_space=pl.ANY),
        out_shape=jax.ShapeDtypeStruct((inner, width), jnp.bfloat16),
        scratch_shapes=[pltpu.VMEM((SLOTS, step, width), jnp.bfloat16), pltpu.SemaphoreType.DMA((SLOTS,))],
        compiler_params=pltpu.CompilerParams(vmem_limit_bytes=SMALL_MIB << 20),
        cost_estimate=pl.CostEstimate(
            flops=2 * inner * width * rows, bytes_accessed=2 * inner * width, transcendentals=0
        ),
    )(x, g)


def swap(value, axis, size, offset):
    rows = value.shape[0]
    spare = -rows % 8
    if spare:
        value = jnp.concatenate([value, jnp.zeros((spare,) + value.shape[1:], value.dtype)], axis=0)
    return lax.ppermute(value, axis, [(i, i ^ offset) for i in range(size)])[:rows]


def per_device(tokens, out_grad, routes, gate_probs, hot, gate_weight, up_weight, down_weight):
    groups = lax.axis_size("group")
    slices = lax.axis_size("ep")
    width = tokens.shape[1]
    half = width // 2
    block = groups * CAP
    bits = slices.bit_length() - 1
    order_a = list(range(bits - 1, -1, -1))
    order_b = [0] + list(range(bits - 1, 0, -1))
    masks_a, masks_b = masks_of(order_a), masks_of(order_b)

    experts = jnp.arange(groups, dtype=jnp.int32) ^ lax.axis_index("group")
    onehot, slot_weight = slot_map(routes, gate_probs, experts, CAP)
    hot_id = jnp.remainder(hot[0], groups)
    slot_ids = jnp.arange(CAP, dtype=jnp.int32)
    retained = ((experts == hot_id)[:, None] | (slot_ids[None, :] < COLD_CAP)).astype(jnp.float32)
    pick = onehot * retained[:, :, None]
    weight = slot_weight * retained
    picker = pick.astype(jnp.bfloat16)
    token_slots = jnp.einsum("est,td->esd", picker, tokens, preferred_element_type=jnp.float32).astype(jnp.bfloat16)
    picked = jnp.einsum("est,td->esd", picker, out_grad, preferred_element_type=jnp.float32)
    signal_slots = (weight[:, :, None] * picked).astype(jnp.bfloat16)
    def exchange(slots):
        own = jnp.concatenate([slots[0]] + [swap(slots[k], "group", groups, k) for k in range(1, groups)], axis=0)
        return (own[:, :half], own[:, half:])

    def send(held, stage):
        return tuple(swap(x, "ep", slices, 1 << order[stage]) for x, order in zip(held, (order_a, order_b)))

    def grow(held, got):
        return tuple(jnp.concatenate([x, y], axis=0) for x, y in zip(held, got))

    back = np.zeros((slices * block,) * 2, np.float32)
    for at, mask in enumerate(masks_b):
        for row in range(block):
            back[at * block + row, masks_a.index(mask) * block + row] = 1.0
    perm = jnp.asarray(back.T, jnp.bfloat16)
    back = jnp.asarray(back, jnp.bfloat16)

    wg = jnp.swapaxes(gate_weight[0], 0, 1)
    wu = jnp.swapaxes(up_weight[0], 0, 1)
    wd = down_weight[0]
    tie = lax.optimization_barrier

    held_t, held_s = exchange(token_slots), exchange(signal_slots)
    weights, loaded = [wg, wu], []
    held_t, weights = tie((held_t, weights))
    for stage in range(bits - 1):
        got_t = send(held_t, stage)
        if len(loaded) < 2:
            loaded.append(load_call(weights[len(loaded)], len(loaded)))
        held_t = grow(held_t, got_t)
        held_t, loaded, weights = tie((held_t, loaded, weights))
    held_t, held_s = tie((held_t, held_s))
    got_t = send(held_t, bits - 1)
    got_s = send(held_s, 0)
    for stage in range(1, bits - 2):
        held_s = grow(held_s, got_s)
        got_s = send(held_s, stage)
    held_s = grow(held_s, got_s)
    wg, wu_here = loaded
    held_t, got_t, held_s, wg, wu_here = tie((held_t, got_t, held_s, wg, wu_here))
    parts_t = (held_t[0], got_t[0], held_t[1], got_t[1])
    got_s = send(held_s, bits - 2)
    t, pg = gate_call(perm, parts_t, wg)
    held_s = grow(held_s, got_s)
    t, pg, held_s = tie((t, pg, held_s))
    got_s = send(held_s, bits - 1)
    pu = up_call(t, wu_here)
    pu, held_s, got_s = tie((pu, held_s, got_s))
    parts_s = (held_s[0], got_s[0], held_s[1], got_s[1])
    s, h, gs, us, keepa, senda, keepb, sendb = signal_call(perm, back, parts_s, pg, pu, wg, wu, wd)

    work = [(s, h), (t, gs), (t, us)]
    grads = []
    kept, sent = (keepa, keepb), (senda, sendb)
    for at, stage in enumerate(range(bits - 1, -1, -1)):
        got = send(sent, stage)
        if at < len(work):
            grads.append(weight_call(*work[at]))
        sums = tuple((x.astype(jnp.float32) + y.astype(jnp.float32)).astype(jnp.bfloat16) for x, y in zip(kept, got))
        sums, grads, work = tie((sums, grads, work))
        kept = tuple(x[: x.shape[0] // 2] for x in sums)
        sent = tuple(x[x.shape[0] // 2 :] for x in sums)
    for x, g in work[len(grads) :]:
        grads.append(weight_call(x, g))
    gd, gg, gu = grads
    dxa, dxb = sums
    mine = jnp.concatenate([dxa, dxb], axis=1).reshape(groups, CAP, width)
    returned = jnp.stack([mine[0]] + [swap(mine[k], "group", groups, k) for k in range(1, groups)])
    tokens_grad = jnp.einsum("est,esd->td", picker, returned, preferred_element_type=jnp.float32).astype(jnp.bfloat16)
    return (tokens_grad, jnp.swapaxes(gg, 0, 1)[None], jnp.swapaxes(gu, 0, 1)[None], gd[None])


def solution(mesh):
    in_specs = (
        P(("group", "ep"), None),
        P(("group", "ep"), None),
        P(("group", "ep"), None),
        P(("group", "ep"), None),
        P(),
        P("group", None, "ep"),
        P("group", None, "ep"),
        P("group", "ep", None),
    )
    out_specs = (
        P(("group", "ep"), None),
        P("group", None, "ep"),
        P("group", None, "ep"),
        P("group", "ep", None),
    )
    return jax.shard_map(per_device, mesh=mesh, in_specs=in_specs, out_specs=out_specs, check_vma=False)
```

```python
import functools

import jax
import jax.numpy as jnp
import numpy as np
from jax import lax
from jax.experimental import pallas as pl
from jax.experimental.pallas import tpu as pltpu
from jax.sharding import PartitionSpec as P

CAP = 5
COLD_CAP = 3
SLOTS = 3
STEP = 512
AHEAD = 4
SIGNAL_MIB = 44
SMALL_MIB = 12

NT = (((1,), (1,)), ((), ()))
TN = (((0,), (0,)), ((), ()))
NN = (((1,), (0,)), ((), ()))


def mm(left, right, dims):
    return lax.dot_general(left, right, dims, preferred_element_type=jnp.float32)


def tile_of(inner, limit=344):
    fits = [t for t in range(8, limit + 1, 8) if inner % t == 0]
    return fits[-1] if fits else inner


def slot_map(route_block, prob_block, expert_index, capacity):
    named_hits = route_block[None, :, :] == expert_index[:, None, None]
    weight_sum = jnp.sum(jnp.where(named_hits, prob_block[None, :, :], 0.0), axis=2)
    chosen = jnp.any(named_hits, axis=2).astype(jnp.int32)
    position = jnp.cumsum(chosen, axis=1) - 1
    slot_index = jnp.arange(capacity, dtype=jnp.int32)
    onehot = (
        (position[:, None, :] == slot_index[None, :, None]) & (chosen[:, None, :] == 1)
    ).astype(jnp.float32)
    slot_weight = jnp.sum(onehot * weight_sum[:, None, :], axis=2)
    return (onehot, slot_weight)


def full(shape):
    return pl.BlockSpec(shape, lambda i: (0,) * len(shape), pipeline_mode=pl.Buffered(1))


def rows_of(tile, width):
    return pl.BlockSpec((tile, width), lambda i: (i, 0))


def masks_of(bits):
    masks = [0]
    for bit in bits:
        masks = masks + [m | (1 << bit) for m in masks]
    return masks


def join(perm, refs):
    a0, a1, b0, b1 = (ref[...] for ref in refs)
    late = mm(perm, jnp.concatenate([b0, b1], axis=0), NN).astype(jnp.bfloat16)
    return jnp.concatenate([jnp.concatenate([a0, a1], axis=0), late], axis=1)


def cuts_of(inner, step):
    return [(low, min(low + step, inner)) for low in range(0, inner, step)]


VMEM = pl.BlockSpec(memory_space=pltpu.VMEM)
ANY = pl.BlockSpec(memory_space=pl.ANY)


def load_kernel(cuts, w_hbm, w_ref, sems):
    copies = []
    for at, (low, high) in enumerate(cuts):
        rows = pl.ds(low, high - low)
        copies.append(pltpu.make_async_copy(w_hbm.at[rows, :], w_ref.at[rows, :], sems.at[at]))
        copies[at].start()
    for copy in copies:
        copy.wait()


def load_call(w, before):
    size = 2 * w.size
    grant = (63 << 20) - (before + 1) * size - min(6 << 20, size // 2)
    cuts = cuts_of(w.shape[0], 344)
    return pl.pallas_call(
        functools.partial(load_kernel, cuts),
        in_specs=[pl.BlockSpec(memory_space=pltpu.HBM)],
        out_specs=VMEM,
        out_shape=pltpu.VMEM(w.shape, w.dtype),
        scratch_shapes=[pltpu.SemaphoreType.DMA((len(cuts),))],
        compiler_params=pltpu.CompilerParams(vmem_limit_bytes=grant),
        cost_estimate=pl.CostEstimate(flops=0, bytes_accessed=2 * w.size, transcendentals=0),
    )(w)


def gate_kernel(cuts, perm_ref, a0_ref, a1_ref, b0_ref, b1_ref, wg_ref, t_ref, pg_ref):
    t = join(perm_ref[...], (a0_ref, a1_ref, b0_ref, b1_ref))
    t_ref[...] = t
    for low, high in cuts:
        pg_ref[low:high, :] = mm(wg_ref[low:high, :], t, NT)


def gate_call(perm, parts, wg):
    inner, width = wg.shape
    rows = perm.shape[0]
    return pl.pallas_call(
        functools.partial(gate_kernel, cuts_of(inner, STEP)),
        in_specs=[VMEM] * 6,
        out_specs=[VMEM] * 2,
        out_shape=[
            jax.ShapeDtypeStruct((rows, width), jnp.bfloat16),
            jax.ShapeDtypeStruct((inner, rows), jnp.float32),
        ],
        compiler_params=pltpu.CompilerParams(vmem_limit_bytes=SMALL_MIB << 20),
        cost_estimate=pl.CostEstimate(
            flops=2 * inner * width * rows, bytes_accessed=2 * inner * width, transcendentals=0
        ),
    )(perm, *parts, wg)


def up_kernel(cuts, t_ref, wu_ref, pu_ref):
    t = t_ref[...]
    for low, high in cuts:
        pu_ref[low:high, :] = mm(wu_ref[low:high, :], t, NT)


def up_call(t, wu):
    inner, width = wu.shape
    rows = t.shape[0]
    return pl.pallas_call(
        functools.partial(up_kernel, cuts_of(inner, STEP)),
        in_specs=[VMEM] * 2,
        out_specs=VMEM,
        out_shape=jax.ShapeDtypeStruct((inner, rows), jnp.float32),
        compiler_params=pltpu.CompilerParams(vmem_limit_bytes=SMALL_MIB << 20),
        cost_estimate=pl.CostEstimate(
            flops=2 * inner * width * rows, bytes_accessed=2 * inner * width, transcendentals=0
        ),
    )(t, wu)


def signal_kernel(
    cuts, perm_ref, back_ref, a0_ref, a1_ref, b0_ref, b1_ref, pg_ref, pu_ref, wg_hbm, wu_hbm, wd_hbm,
    s_ref, h_ref, gs_ref, us_ref, keepa_ref, senda_ref, keepb_ref, sendb_ref, both_ref, w_ref, wd_ref, acc_ref, sems,
):
    copies = []
    for at, (low, high) in enumerate(cuts):
        rows = pl.ds(low, high - low)
        copies.append(pltpu.make_async_copy(wd_hbm.at[rows, :], wd_ref.at[rows, :], sems.at[0, at]))
    for at, (low, high) in enumerate(cuts):
        size = high - low
        for side, src in enumerate((wg_hbm, wu_hbm)):
            dst = w_ref.at[pl.ds(2 * low + side * size, size), :]
            copies.append(pltpu.make_async_copy(src.at[pl.ds(low, size), :], dst, sems.at[1 + side, at]))
    for copy in copies[:AHEAD]:
        copy.start()

    def arrive(at):
        copies[at].wait()
        if at + AHEAD < len(copies):
            copies[at + AHEAD].start()

    s_ref[...] = join(perm_ref[...], (a0_ref, a1_ref, b0_ref, b1_ref))
    s = s_ref[...]
    for at, (low, high) in enumerate(cuts):
        size = high - low
        gate = pg_ref[low:high, :]
        up = pu_ref[low:high, :]
        logistic = jax.nn.sigmoid(gate)
        swished = gate * logistic
        h_ref[low:high, :] = (swished * up).astype(jnp.bfloat16)
        arrive(at)
        hidden_grad = mm(wd_ref[low:high, :], s, NT)
        gs = (hidden_grad * up * logistic * (1.0 + gate * (1.0 - logistic))).astype(jnp.bfloat16)
        us = (hidden_grad * swished).astype(jnp.bfloat16)
        gs_ref[low:high, :] = gs
        us_ref[low:high, :] = us
        both_ref[2 * low : 2 * low + size, :] = gs
        both_ref[2 * low + size : 2 * high, :] = us
    half = keepa_ref.shape[1]
    kept = keepa_ref.shape[0]
    for at, (low, high) in enumerate(cuts):
        arrive(len(cuts) + 2 * at)
        arrive(len(cuts) + 2 * at + 1)
        part = mm(both_ref[2 * low : 2 * high, :], w_ref[2 * low : 2 * high, :], TN)
        if at > 0:
            part = acc_ref[...] + part
        if at < len(cuts) - 1:
            acc_ref[...] = part
        else:
            first = part[:, :half].astype(jnp.bfloat16)
            keepa_ref[...] = first[:kept]
            senda_ref[...] = first[kept:]
            late = mm(back_ref[...], part[:, half:].astype(jnp.bfloat16), NN).astype(jnp.bfloat16)
            keepb_ref[...] = late[:kept]
            sendb_ref[...] = late[kept:]


def signal_call(perm, back, parts, pg, pu, wg, wu, wd):
    inner, width = wg.shape
    rows = perm.shape[0]
    cuts = cuts_of(inner, STEP)
    vmem = pl.BlockSpec(memory_space=pltpu.VMEM)
    hbm = pl.BlockSpec(memory_space=pl.ANY)
    return pl.pallas_call(
        functools.partial(signal_kernel, cuts),
        in_specs=[vmem] * 8 + [hbm] * 3,
        out_specs=[vmem] * 8,
        out_shape=[jax.ShapeDtypeStruct((rows, width), jnp.bfloat16)]
        + [jax.ShapeDtypeStruct((inner, rows), jnp.bfloat16)] * 3
        + [jax.ShapeDtypeStruct((rows // 2, width // 2), jnp.bfloat16)] * 4,
        scratch_shapes=[
            pltpu.VMEM((2 * inner, rows), jnp.bfloat16),
            pltpu.VMEM((2 * inner, width), jnp.bfloat16),
            pltpu.VMEM((inner, width), jnp.bfloat16),
            pltpu.VMEM((rows, width), jnp.float32),
            pltpu.SemaphoreType.DMA((3, len(cuts))),
        ],
        compiler_params=pltpu.CompilerParams(vmem_limit_bytes=SIGNAL_MIB << 20),
        cost_estimate=pl.CostEstimate(
            flops=6 * inner * width * rows, bytes_accessed=6 * inner * width, transcendentals=inner * rows
        ),
    )(perm, back, *parts, pg, pu, wg, wu, wd)


def weight_kernel(cuts, x_ref, g_ref, out_hbm, buf_ref, sems):
    x = x_ref[...]
    copies = []
    for at, (low, high) in enumerate(cuts):
        slot = at % SLOTS
        if at >= SLOTS:
            copies[at - SLOTS].wait()
        size = high - low
        buf_ref[slot, :size, :] = mm(g_ref[low:high, :], x, NN).astype(jnp.bfloat16)
        copies.append(
            pltpu.make_async_copy(buf_ref.at[slot, pl.ds(0, size), :], out_hbm.at[pl.ds(low, size), :], sems.at[slot])
        )
        copies[at].start()
    for copy in copies[max(0, len(copies) - SLOTS) :]:
        copy.wait()


def weight_call(x, g):
    inner, rows = g.shape
    width = x.shape[1]
    step = min(256, inner)
    cuts = cuts_of(inner, step)
    return pl.pallas_call(
        functools.partial(weight_kernel, cuts),
        in_specs=[pl.BlockSpec(memory_space=pltpu.VMEM)] * 2,
        out_specs=pl.BlockSpec(memory_space=pl.ANY),
        out_shape=jax.ShapeDtypeStruct((inner, width), jnp.bfloat16),
        scratch_shapes=[pltpu.VMEM((SLOTS, step, width), jnp.bfloat16), pltpu.SemaphoreType.DMA((SLOTS,))],
        compiler_params=pltpu.CompilerParams(vmem_limit_bytes=SMALL_MIB << 20),
        cost_estimate=pl.CostEstimate(
            flops=2 * inner * width * rows, bytes_accessed=2 * inner * width, transcendentals=0
        ),
    )(x, g)


def swap(value, axis, size, offset):
    rows = value.shape[0]
    spare = -rows % 8
    if spare:
        value = jnp.concatenate([value, jnp.zeros((spare,) + value.shape[1:], value.dtype)], axis=0)
    return lax.ppermute(value, axis, [(i, i ^ offset) for i in range(size)])[:rows]


def per_device(tokens, out_grad, routes, gate_probs, hot, gate_weight, up_weight, down_weight):
    groups = lax.axis_size("group")
    slices = lax.axis_size("ep")
    width = tokens.shape[1]
    half = width // 2
    block = groups * CAP
    bits = slices.bit_length() - 1
    order_a = list(range(bits - 1, -1, -1))
    order_b = [0] + list(range(bits - 1, 0, -1))
    masks_a, masks_b = masks_of(order_a), masks_of(order_b)

    experts = jnp.arange(groups, dtype=jnp.int32) ^ lax.axis_index("group")
    onehot, slot_weight = slot_map(routes, gate_probs, experts, CAP)
    hot_id = jnp.remainder(hot[0], groups)
    slot_ids = jnp.arange(CAP, dtype=jnp.int32)
    retained = ((experts == hot_id)[:, None] | (slot_ids[None, :] < COLD_CAP)).astype(jnp.float32)
    pick = onehot * retained[:, :, None]
    weight = slot_weight * retained
    picker = pick.astype(jnp.bfloat16)
    token_slots = jnp.einsum("est,td->esd", picker, tokens, preferred_element_type=jnp.float32).astype(jnp.bfloat16)
    picked = jnp.einsum("est,td->esd", picker, out_grad, preferred_element_type=jnp.float32)
    signal_slots = (weight[:, :, None] * picked).astype(jnp.bfloat16)
    def exchange(slots):
        own = jnp.concatenate([slots[0]] + [swap(slots[k], "group", groups, k) for k in range(1, groups)], axis=0)
        return (own[:, :half], own[:, half:])

    def send(held, stage):
        return tuple(swap(x, "ep", slices, 1 << order[stage]) for x, order in zip(held, (order_a, order_b)))

    def grow(held, got):
        return tuple(jnp.concatenate([x, y], axis=0) for x, y in zip(held, got))

    back = np.zeros((slices * block,) * 2, np.float32)
    for at, mask in enumerate(masks_b):
        for row in range(block):
            back[at * block + row, masks_a.index(mask) * block + row] = 1.0
    perm = jnp.asarray(back.T, jnp.bfloat16)
    back = jnp.asarray(back, jnp.bfloat16)

    wg = jnp.swapaxes(gate_weight[0], 0, 1)
    wu = jnp.swapaxes(up_weight[0], 0, 1)
    wd = down_weight[0]
    tie = lax.optimization_barrier

    held_t, held_s = exchange(token_slots), exchange(signal_slots)
    weights, loaded = [wg, wu], []
    held_t, weights = tie((held_t, weights))
    for stage in range(bits - 1):
        got_t = send(held_t, stage)
        if len(loaded) < 2:
            loaded.append(load_call(weights[len(loaded)], len(loaded)))
        held_t = grow(held_t, got_t)
        held_t, loaded, weights = tie((held_t, loaded, weights))
    held_t, held_s = tie((held_t, held_s))
    got_t = send(held_t, bits - 1)
    got_s = send(held_s, 0)
    for stage in range(1, bits - 2):
        held_s = grow(held_s, got_s)
        got_s = send(held_s, stage)
    held_s = grow(held_s, got_s)
    held_t, got_t, held_s, wg_here, wu_here = tie((held_t, got_t, held_s, *loaded))
    parts_t = (held_t[0], got_t[0], held_t[1], got_t[1])
    got_s = send(held_s, bits - 2)
    t, pg = gate_call(perm, parts_t, wg_here)
    held_s = grow(held_s, got_s)
    t, pg, held_s = tie((t, pg, held_s))
    got_s = send(held_s, bits - 1)
    pu = up_call(t, wu_here)
    pu, held_s, got_s = tie((pu, held_s, got_s))
    parts_s = (held_s[0], got_s[0], held_s[1], got_s[1])
    s, h, gs, us, keepa, senda, keepb, sendb = signal_call(perm, back, parts_s, pg, pu, wg, wu, wd)

    work = [(s, h), (t, gs), (t, us)]
    grads = []
    kept, sent = (keepa, keepb), (senda, sendb)
    for at, stage in enumerate(range(bits - 1, -1, -1)):
        got = send(sent, stage)
        for _ in range(2 if at == 0 else 1):
            if len(grads) < len(work):
                grads.append(weight_call(*work[len(grads)]))
        sums = tuple((x.astype(jnp.float32) + y.astype(jnp.float32)).astype(jnp.bfloat16) for x, y in zip(kept, got))
        sums, grads, work = tie((sums, grads, work))
        kept = tuple(x[: x.shape[0] // 2] for x in sums)
        sent = tuple(x[x.shape[0] // 2 :] for x in sums)
    for x, g in work[len(grads) :]:
        grads.append(weight_call(x, g))
    gd, gg, gu = grads
    dxa, dxb = sums
    mine = jnp.concatenate([dxa, dxb], axis=1).reshape(groups, CAP, width)
    returned = jnp.stack([mine[0]] + [swap(mine[k], "group", groups, k) for k in range(1, groups)])
    tokens_grad = jnp.einsum("est,esd->td", picker, returned, preferred_element_type=jnp.float32).astype(jnp.bfloat16)
    return (tokens_grad, jnp.swapaxes(gg, 0, 1)[None], jnp.swapaxes(gu, 0, 1)[None], gd[None])


def solution(mesh):
    in_specs = (
        P(("group", "ep"), None),
        P(("group", "ep"), None),
        P(("group", "ep"), None),
        P(("group", "ep"), None),
        P(),
        P("group", None, "ep"),
        P("group", None, "ep"),
        P("group", "ep", None),
    )
    out_specs = (
        P(("group", "ep"), None),
        P("group", None, "ep"),
        P("group", None, "ep"),
        P("group", "ep", None),
    )
    return jax.shard_map(per_device, mesh=mesh, in_specs=in_specs, out_specs=out_specs, check_vma=False)
```

```python
import functools

import jax
import jax.numpy as jnp
import numpy as np
from jax import lax
from jax.experimental import pallas as pl
from jax.experimental.pallas import tpu as pltpu
from jax.sharding import PartitionSpec as P

CAP = 5
COLD_CAP = 3
SLOTS = 3
STEP = 512
AHEAD = 4
SIGNAL_MIB = 28
SMALL_MIB = 12

NT = (((1,), (1,)), ((), ()))
TN = (((0,), (0,)), ((), ()))
NN = (((1,), (0,)), ((), ()))


def mm(left, right, dims):
    return lax.dot_general(left, right, dims, preferred_element_type=jnp.float32)


def tile_of(inner, limit=344):
    fits = [t for t in range(8, limit + 1, 8) if inner % t == 0]
    return fits[-1] if fits else inner


def slot_map(route_block, prob_block, expert_index, capacity):
    named_hits = route_block[None, :, :] == expert_index[:, None, None]
    weight_sum = jnp.sum(jnp.where(named_hits, prob_block[None, :, :], 0.0), axis=2)
    chosen = jnp.any(named_hits, axis=2).astype(jnp.int32)
    position = jnp.cumsum(chosen, axis=1) - 1
    slot_index = jnp.arange(capacity, dtype=jnp.int32)
    onehot = (
        (position[:, None, :] == slot_index[None, :, None]) & (chosen[:, None, :] == 1)
    ).astype(jnp.float32)
    slot_weight = jnp.sum(onehot * weight_sum[:, None, :], axis=2)
    return (onehot, slot_weight)


def full(shape):
    return pl.BlockSpec(shape, lambda i: (0,) * len(shape), pipeline_mode=pl.Buffered(1))


def rows_of(tile, width):
    return pl.BlockSpec((tile, width), lambda i: (i, 0))


def masks_of(bits):
    masks = [0]
    for bit in bits:
        masks = masks + [m | (1 << bit) for m in masks]
    return masks


def join(perm, refs):
    a0, a1, b0, b1 = (ref[...] for ref in refs)
    late = mm(perm, jnp.concatenate([b0, b1], axis=0), NN).astype(jnp.bfloat16)
    return jnp.concatenate([jnp.concatenate([a0, a1], axis=0), late], axis=1)


def cuts_of(inner, step):
    return [(low, min(low + step, inner)) for low in range(0, inner, step)]


VMEM = pl.BlockSpec(memory_space=pltpu.VMEM)
ANY = pl.BlockSpec(memory_space=pl.ANY)


def load_kernel(cuts, w_hbm, w_ref, sems):
    copies = []
    for at, (low, high) in enumerate(cuts):
        rows = pl.ds(low, high - low)
        copies.append(pltpu.make_async_copy(w_hbm.at[rows, :], w_ref.at[rows, :], sems.at[at]))
        copies[at].start()
    for copy in copies:
        copy.wait()


def load_call(w, before):
    size = 2 * w.size
    grant = (63 << 20) - (before + 1) * size - min(6 << 20, size // 2)
    cuts = cuts_of(w.shape[0], 344)
    return pl.pallas_call(
        functools.partial(load_kernel, cuts),
        in_specs=[pl.BlockSpec(memory_space=pltpu.HBM)],
        out_specs=VMEM,
        out_shape=pltpu.VMEM(w.shape, w.dtype),
        scratch_shapes=[pltpu.SemaphoreType.DMA((len(cuts),))],
        compiler_params=pltpu.CompilerParams(vmem_limit_bytes=grant),
        cost_estimate=pl.CostEstimate(flops=0, bytes_accessed=2 * w.size, transcendentals=0),
    )(w)


def gate_kernel(cuts, perm_ref, a0_ref, a1_ref, b0_ref, b1_ref, wg_ref, t_ref, pg_ref):
    t = join(perm_ref[...], (a0_ref, a1_ref, b0_ref, b1_ref))
    t_ref[...] = t
    for low, high in cuts:
        pg_ref[low:high, :] = mm(wg_ref[low:high, :], t, NT)


def gate_call(perm, parts, wg):
    inner, width = wg.shape
    rows = perm.shape[0]
    return pl.pallas_call(
        functools.partial(gate_kernel, cuts_of(inner, STEP)),
        in_specs=[VMEM] * 6,
        out_specs=[VMEM] * 2,
        out_shape=[
            jax.ShapeDtypeStruct((rows, width), jnp.bfloat16),
            jax.ShapeDtypeStruct((inner, rows), jnp.float32),
        ],
        compiler_params=pltpu.CompilerParams(vmem_limit_bytes=SMALL_MIB << 20),
        cost_estimate=pl.CostEstimate(
            flops=2 * inner * width * rows, bytes_accessed=2 * inner * width, transcendentals=0
        ),
    )(perm, *parts, wg)


def up_kernel(cuts, t_ref, wu_ref, pu_ref):
    t = t_ref[...]
    for low, high in cuts:
        pu_ref[low:high, :] = mm(wu_ref[low:high, :], t, NT)


def up_call(t, wu):
    inner, width = wu.shape
    rows = t.shape[0]
    return pl.pallas_call(
        functools.partial(up_kernel, cuts_of(inner, STEP)),
        in_specs=[VMEM] * 2,
        out_specs=VMEM,
        out_shape=jax.ShapeDtypeStruct((inner, rows), jnp.float32),
        compiler_params=pltpu.CompilerParams(vmem_limit_bytes=SMALL_MIB << 20),
        cost_estimate=pl.CostEstimate(
            flops=2 * inner * width * rows, bytes_accessed=2 * inner * width, transcendentals=0
        ),
    )(t, wu)


def signal_kernel(
    cuts, perm_ref, back_ref, a0_ref, a1_ref, b0_ref, b1_ref, pg_ref, pu_ref, wd_ref, wg_hbm, wu_hbm,
    s_ref, h_ref, gs_ref, us_ref, keepa_ref, senda_ref, keepb_ref, sendb_ref, both_ref, w_ref, acc_ref, sems,
):
    copies = []
    for at, (low, high) in enumerate(cuts):
        size = high - low
        for side, src in enumerate((wg_hbm, wu_hbm)):
            dst = w_ref.at[pl.ds(2 * low + side * size, size), :]
            copies.append(pltpu.make_async_copy(src.at[pl.ds(low, size), :], dst, sems.at[side, at]))
    for copy in copies[:AHEAD]:
        copy.start()

    def arrive(at):
        copies[at].wait()
        if at + AHEAD < len(copies):
            copies[at + AHEAD].start()

    s_ref[...] = join(perm_ref[...], (a0_ref, a1_ref, b0_ref, b1_ref))
    s = s_ref[...]
    for at, (low, high) in enumerate(cuts):
        size = high - low
        gate = pg_ref[low:high, :]
        up = pu_ref[low:high, :]
        logistic = jax.nn.sigmoid(gate)
        swished = gate * logistic
        h_ref[low:high, :] = (swished * up).astype(jnp.bfloat16)
        hidden_grad = mm(wd_ref[low:high, :], s, NT)
        gs = (hidden_grad * up * logistic * (1.0 + gate * (1.0 - logistic))).astype(jnp.bfloat16)
        us = (hidden_grad * swished).astype(jnp.bfloat16)
        gs_ref[low:high, :] = gs
        us_ref[low:high, :] = us
        both_ref[2 * low : 2 * low + size, :] = gs
        both_ref[2 * low + size : 2 * high, :] = us
    half = keepa_ref.shape[1]
    kept = keepa_ref.shape[0]
    for at, (low, high) in enumerate(cuts):
        arrive(2 * at)
        arrive(2 * at + 1)
        part = mm(both_ref[2 * low : 2 * high, :], w_ref[2 * low : 2 * high, :], TN)
        if at > 0:
            part = acc_ref[...] + part
        if at < len(cuts) - 1:
            acc_ref[...] = part
        else:
            first = part[:, :half].astype(jnp.bfloat16)
            keepa_ref[...] = first[:kept]
            senda_ref[...] = first[kept:]
            late = mm(back_ref[...], part[:, half:].astype(jnp.bfloat16), NN).astype(jnp.bfloat16)
            keepb_ref[...] = late[:kept]
            sendb_ref[...] = late[kept:]


def signal_call(perm, back, parts, pg, pu, wg, wu, wd):
    inner, width = wg.shape
    rows = perm.shape[0]
    cuts = cuts_of(inner, STEP)
    vmem = pl.BlockSpec(memory_space=pltpu.VMEM)
    hbm = pl.BlockSpec(memory_space=pl.ANY)
    return pl.pallas_call(
        functools.partial(signal_kernel, cuts),
        in_specs=[vmem] * 9 + [hbm] * 2,
        out_specs=[vmem] * 8,
        out_shape=[jax.ShapeDtypeStruct((rows, width), jnp.bfloat16)]
        + [jax.ShapeDtypeStruct((inner, rows), jnp.bfloat16)] * 3
        + [jax.ShapeDtypeStruct((rows // 2, width // 2), jnp.bfloat16)] * 4,
        scratch_shapes=[
            pltpu.VMEM((2 * inner, rows), jnp.bfloat16),
            pltpu.VMEM((2 * inner, width), jnp.bfloat16),
            pltpu.VMEM((rows, width), jnp.float32),
            pltpu.SemaphoreType.DMA((2, len(cuts))),
        ],
        compiler_params=pltpu.CompilerParams(vmem_limit_bytes=SIGNAL_MIB << 20),
        cost_estimate=pl.CostEstimate(
            flops=6 * inner * width * rows, bytes_accessed=6 * inner * width, transcendentals=inner * rows
        ),
    )(perm, back, *parts, pg, pu, wd, wg, wu)


def weight_kernel(cuts, x_ref, g_ref, out_hbm, buf_ref, sems):
    x = x_ref[...]
    copies = []
    for at, (low, high) in enumerate(cuts):
        slot = at % SLOTS
        if at >= SLOTS:
            copies[at - SLOTS].wait()
        size = high - low
        buf_ref[slot, :size, :] = mm(g_ref[low:high, :], x, NN).astype(jnp.bfloat16)
        copies.append(
            pltpu.make_async_copy(buf_ref.at[slot, pl.ds(0, size), :], out_hbm.at[pl.ds(low, size), :], sems.at[slot])
        )
        copies[at].start()
    for copy in copies[max(0, len(copies) - SLOTS) :]:
        copy.wait()


def weight_call(x, g):
    inner, rows = g.shape
    width = x.shape[1]
    step = min(256, inner)
    cuts = cuts_of(inner, step)
    return pl.pallas_call(
        functools.partial(weight_kernel, cuts),
        in_specs=[pl.BlockSpec(memory_space=pltpu.VMEM)] * 2,
        out_specs=pl.BlockSpec(memory_space=pl.ANY),
        out_shape=jax.ShapeDtypeStruct((inner, width), jnp.bfloat16),
        scratch_shapes=[pltpu.VMEM((SLOTS, step, width), jnp.bfloat16), pltpu.SemaphoreType.DMA((SLOTS,))],
        compiler_params=pltpu.CompilerParams(vmem_limit_bytes=SMALL_MIB << 20),
        cost_estimate=pl.CostEstimate(
            flops=2 * inner * width * rows, bytes_accessed=2 * inner * width, transcendentals=0
        ),
    )(x, g)


def swap(value, axis, size, offset):
    rows = value.shape[0]
    spare = -rows % 8
    if spare:
        value = jnp.concatenate([value, jnp.zeros((spare,) + value.shape[1:], value.dtype)], axis=0)
    return lax.ppermute(value, axis, [(i, i ^ offset) for i in range(size)])[:rows]


def per_device(tokens, out_grad, routes, gate_probs, hot, gate_weight, up_weight, down_weight):
    groups = lax.axis_size("group")
    slices = lax.axis_size("ep")
    width = tokens.shape[1]
    half = width // 2
    block = groups * CAP
    bits = slices.bit_length() - 1
    order_a = list(range(bits - 1, -1, -1))
    order_b = [0] + list(range(bits - 1, 0, -1))
    masks_a, masks_b = masks_of(order_a), masks_of(order_b)

    experts = jnp.arange(groups, dtype=jnp.int32) ^ lax.axis_index("group")
    onehot, slot_weight = slot_map(routes, gate_probs, experts, CAP)
    hot_id = jnp.remainder(hot[0], groups)
    slot_ids = jnp.arange(CAP, dtype=jnp.int32)
    retained = ((experts == hot_id)[:, None] | (slot_ids[None, :] < COLD_CAP)).astype(jnp.float32)
    pick = onehot * retained[:, :, None]
    weight = slot_weight * retained
    picker = pick.astype(jnp.bfloat16)
    token_slots = jnp.einsum("est,td->esd", picker, tokens, preferred_element_type=jnp.float32).astype(jnp.bfloat16)
    picked = jnp.einsum("est,td->esd", picker, out_grad, preferred_element_type=jnp.float32)
    signal_slots = (weight[:, :, None] * picked).astype(jnp.bfloat16)
    def exchange(slots):
        own = jnp.concatenate([slots[0]] + [swap(slots[k], "group", groups, k) for k in range(1, groups)], axis=0)
        return (own[:, :half], own[:, half:])

    def send(held, stage):
        return tuple(swap(x, "ep", slices, 1 << order[stage]) for x, order in zip(held, (order_a, order_b)))

    def grow(held, got):
        return tuple(jnp.concatenate([x, y], axis=0) for x, y in zip(held, got))

    back = np.zeros((slices * block,) * 2, np.float32)
    for at, mask in enumerate(masks_b):
        for row in range(block):
            back[at * block + row, masks_a.index(mask) * block + row] = 1.0
    perm = jnp.asarray(back.T, jnp.bfloat16)
    back = jnp.asarray(back, jnp.bfloat16)

    wg = jnp.swapaxes(gate_weight[0], 0, 1)
    wu = jnp.swapaxes(up_weight[0], 0, 1)
    wd = down_weight[0]
    tie = lax.optimization_barrier

    held_t, held_s = exchange(token_slots), exchange(signal_slots)
    weights, loaded = [wg, wu], []
    held_t, weights = tie((held_t, weights))
    for stage in range(bits - 1):
        got_t = send(held_t, stage)
        if len(loaded) < 2:
            loaded.append(load_call(weights[len(loaded)], len(loaded)))
        held_t = grow(held_t, got_t)
        held_t, loaded, weights = tie((held_t, loaded, weights))
    held_t, held_s = tie((held_t, held_s))
    got_t = send(held_t, bits - 1)
    got_s = send(held_s, 0)
    for stage in range(1, bits - 2):
        held_s = grow(held_s, got_s)
        got_s = send(held_s, stage)
    held_s = grow(held_s, got_s)
    held_t, got_t, held_s, wg_here, wu_here = tie((held_t, got_t, held_s, *loaded))
    parts_t = (held_t[0], got_t[0], held_t[1], got_t[1])
    got_s = send(held_s, bits - 2)
    t, pg = gate_call(perm, parts_t, wg_here)
    held_s = grow(held_s, got_s)
    t, pg, held_s = tie((t, pg, held_s))
    got_s = send(held_s, bits - 1)
    pu = up_call(t, wu_here)
    pu, wd = tie((pu, wd))
    pu, held_s, got_s, wd = tie((pu, held_s, got_s, load_call(wd, 0)))
    parts_s = (held_s[0], got_s[0], held_s[1], got_s[1])
    s, h, gs, us, keepa, senda, keepb, sendb = signal_call(perm, back, parts_s, pg, pu, wg, wu, wd)

    work = [(s, h), (t, gs), (t, us)]
    grads = []
    kept, sent = (keepa, keepb), (senda, sendb)
    for at, stage in enumerate(range(bits - 1, -1, -1)):
        got = send(sent, stage)
        for _ in range(2 if at == 0 else 1):
            if len(grads) < len(work):
                grads.append(weight_call(*work[len(grads)]))
        sums = tuple((x.astype(jnp.float32) + y.astype(jnp.float32)).astype(jnp.bfloat16) for x, y in zip(kept, got))
        sums, grads, work = tie((sums, grads, work))
        kept = tuple(x[: x.shape[0] // 2] for x in sums)
        sent = tuple(x[x.shape[0] // 2 :] for x in sums)
    for x, g in work[len(grads) :]:
        grads.append(weight_call(x, g))
    gd, gg, gu = grads
    dxa, dxb = sums
    mine = jnp.concatenate([dxa, dxb], axis=1).reshape(groups, CAP, width)
    returned = jnp.stack([mine[0]] + [swap(mine[k], "group", groups, k) for k in range(1, groups)])
    tokens_grad = jnp.einsum("est,esd->td", picker, returned, preferred_element_type=jnp.float32).astype(jnp.bfloat16)
    return (tokens_grad, jnp.swapaxes(gg, 0, 1)[None], jnp.swapaxes(gu, 0, 1)[None], gd[None])


def solution(mesh):
    in_specs = (
        P(("group", "ep"), None),
        P(("group", "ep"), None),
        P(("group", "ep"), None),
        P(("group", "ep"), None),
        P(),
        P("group", None, "ep"),
        P("group", None, "ep"),
        P("group", "ep", None),
    )
    out_specs = (
        P(("group", "ep"), None),
        P("group", None, "ep"),
        P("group", None, "ep"),
        P("group", "ep", None),
    )
    return jax.shard_map(per_device, mesh=mesh, in_specs=in_specs, out_specs=out_specs, check_vma=False)
```
